32 devices in a mesh: gx: 2 (over y), gy: 4 (over z), gz: 4 (over x, core).
Axes of the slice: x: 2, y: 2, z: 4, core: 2. Of those that a mesh axis runs over, the one named last changes fastest.
Arguments:
- blocks: float32 [2, 4, 4, 8, 128, 128], P('gx', 'gy', 'gz'), as said below
- columns: int32 [2, 4, 4, 8], replicated, may hold values from -1 to 31, as said below
Outputs:
- purified: float32 [2, 4, 4, 8, 128, 128], P('gx', 'gy', 'gz')
The draws below stay inside these ranges and needn't reach their ends.
Inputs may be any that keep to these rules, and one draw needn't show every extreme that they name: columns[i, 0] is i itself; every other entry is -1 or the number of a cluster that differs from i by one along exactly one of the three dimensions, repeats allowed. `blocks`: a block in a slot whose column is -1 is zero.
All inputs are finite; a program needn't handle non-finite values.
Results may differ from the reference program's by a relative error of at most 0.0003.
Values sent between devices are 32-bit elements; how exact they have to be, the bound alone decides.
A program may use at most 64 MiB of HBM per device.

```python
import math
import jax
import jax.numpy as jnp
from jax import lax

B = 128
K = 8
PURIFY = 1
NX = 2
NY = 4
NZ = 4


def pattern(key):
    clusters = NX * NY * NZ
    cluster_ids = jnp.arange(clusters, dtype=jnp.int32)
    coord_x = cluster_ids // (NY * NZ)
    coord_y = cluster_ids // NZ % NY
    coord_z = cluster_ids % NZ
    heading = jax.random.randint(jax.random.fold_in(key, 11), (clusters, K - 1), 0, 6)
    heading = heading.at[0, 0].set(0)
    step_x = jnp.where(heading == 0, -1, jnp.where(heading == 1, 1, 0))
    step_y = jnp.where(heading == 2, -1, jnp.where(heading == 3, 1, 0))
    step_z = jnp.where(heading == 4, -1, jnp.where(heading == 5, 1, 0))
    near_x = coord_x[:, None] + step_x
    near_y = coord_y[:, None] + step_y
    near_z = coord_z[:, None] + step_z
    inside = (near_x >= 0) & (near_x < NX) & (near_y >= 0) & (near_y < NY) & (near_z >= 0) & (near_z < NZ)
    others = jnp.where(inside, (near_x * NY + near_y) * NZ + near_z, -1)
    joined = jnp.concatenate([cluster_ids[:, None], others], axis=1)
    return joined.astype(jnp.int32).reshape(NX, NY, NZ, K)


def draw_columns(key, part):
    return pattern(jax.random.fold_in(key, 5))


def draw_blocks(key, part):
    pattern_cols = pattern(jax.random.fold_in(key, 5))
    sigma = 0.45 / math.sqrt(K * B)
    shape_all = (NX, NY, NZ, K, B, B)
    noise = jax.random.normal(jax.random.fold_in(key, 21), shape_all, jnp.float32)
    diag_vals = jax.random.uniform(jax.random.fold_in(key, 22), (NX, NY, NZ, B), jnp.float32, 0.2, 0.8)
    values = noise * sigma
    identity = jnp.eye(B, dtype=jnp.float32)
    first_slot = (jnp.arange(K) == 0).astype(jnp.float32)[:, None, None]
    values = values + first_slot * (diag_vals[:, :, :, None, None, :] * identity)
    live = (pattern_cols >= 0)[..., None, None]
    return jnp.where(live, values, 0.0).astype(jnp.float32)


def setup_inputs(seed: int = 0) -> dict:
    keys = jax.random.split(jax.random.key(seed), 3)
    return {
        "blocks": draw_blocks(jax.random.fold_in(keys[2], 71), 0),
        "columns": draw_columns(jax.random.fold_in(keys[2], 71), 0),
    }


exact_mode = lax.Precision.HIGHEST


def purify_once(current, flat_cols):
    flat_blocks = current.reshape(-1, K, B, B)

    def one_row(packed):
        row_blocks, row_cols = packed
        safe_cols = jnp.maximum(row_cols, 0)
        far_rows = flat_blocks[safe_cols]
        far_cols = flat_cols[safe_cols]
        matches = (far_cols[:, :, None] == row_cols[None, None, :]) & (row_cols[None, None, :] >= 0) & (row_cols[:, None, None] >= 0)
        picked = jnp.einsum("tus,tuab->tsab", matches.astype(jnp.float32), far_rows, precision=exact_mode)
        square = jnp.einsum("tab,tsbc->sac", row_blocks, picked, precision=exact_mode)
        cubed = jnp.einsum("tab,tsbc->sac", square, picked, precision=exact_mode)
        return 3.0 * square - 2.0 * cubed

    return lax.map(one_row, (flat_blocks, flat_cols)).reshape(current.shape)


def reference(blocks, columns):
    flat_cols = columns.reshape(-1, K)
    current = blocks
    for sweep in range(PURIFY):
        current = purify_once(current, flat_cols)
    return current
```

```python
import functools
from typing import Any, NamedTuple

import jax
import jax.numpy as jnp
from jax import lax
from jax.experimental import pallas as pl
from jax.experimental.pallas import tpu as pltpu
from jax.sharding import PartitionSpec as P

MESH = pl.DeviceIdType.MESH
AXES = ("gx", "gy", "gz")


def directions(sizes):
    found = []
    for axis, size in enumerate(sizes):
        if size == 2:
            found.append((axis, 0))
        elif size > 2:
            found.extend([(axis, -1), (axis, 1)])
    return found


def halves(value):
    head = value.astype(jnp.bfloat16)
    tail = (value - head.astype(jnp.float32)).astype(jnp.bfloat16)
    return head, tail


def split(value):
    return jnp.concatenate(halves(value), axis=1)


def twice(right):
    return jnp.concatenate([right, right], axis=0)


def dot(left, right):
    return jnp.dot(left, right, preferred_element_type=jnp.float32)


def folded(both):
    width = both.shape[1] // 2
    return both[:, :width] + both[:, width:]


def spread(left, rights):
    width = left.shape[1] // 2
    long = jnp.concatenate([left, left[:, :width]], axis=1)
    found = []
    for at in range(0, len(rights), 2):
        pair = rights[at : at + 2]
        heads = jnp.concatenate([right[:, :width] for right in pair], axis=1)
        tails = jnp.concatenate([right[:, width:] for right in pair], axis=1)
        both = dot(long, jnp.concatenate([heads, heads, tails], axis=0))
        found.extend(both[:, width * k : width * (k + 1)] for k in range(len(pair)))
    return found


class Side(NamedTuple):
    axis: Any
    index: Any
    far_index: Any
    device: Any
    there: Any
    answers: Any


def sides_of(sizes, where):
    dirs = directions(sizes)
    low, high = [], []

    def moved(axis, place):
        return tuple(place if a == axis else at for a, at in enumerate(where))

    for d, (axis, step) in enumerate(dirs):
        if axis == 2:
            continue
        place = where[axis]
        if step == 0:
            low.append(Side(axis, d, d, moved(axis, 1 - place), jnp.bool_(True), place == 1))
        else:
            there = place > 0 if step < 0 else place < sizes[axis] - 1
            to = moved(axis, place + step)
            side = Side(axis, d, dirs.index((axis, -step)), to, there, jnp.bool_(step < 0))
            (low if step < 0 else high).append(side)
    along = [d for d, (axis, _) in enumerate(dirs) if axis == 2]
    odd = lax.rem(where[2], 2)
    pair, cross = [], []
    for up, found in ((1 - odd, pair), (odd, cross)):
        if len(along) == 2:
            place = where[2] + 2 * up - 1
            there = place < sizes[2]
            if found is cross:
                there = jnp.logical_and(there, place >= 0)
            found.append(Side(2, along[0] + up, along[1] - up, moved(2, place), there, odd == 0))
    if len(along) == 1:
        pair.append(Side(2, along[0], along[0], moved(2, 1 - where[2]), jnp.bool_(True), odd == 0))
    return low, high, pair, cross


def urgent_first(sides):
    count = len(sides)
    first = jnp.int32(0)
    for k in reversed(range(count)):
        first = jnp.where(jnp.logical_and(sides[k].there, sides[k].answers), k, first)

    def pick(values, at):
        found = values[0]
        for k in range(1, count):
            found = jnp.where(at == k, values[k], found)
        return found

    turned = []
    for k in range(count):
        at = jnp.where(first + k < count, first + k, first + k - count)
        turned.append(
            Side(
                pick([side.axis for side in sides], at),
                pick([side.index for side in sides], at),
                pick([side.far_index for side in sides], at),
                tuple(pick([side.device[a] for side in sides], at) for a in range(3)),
                pick([side.there.astype(jnp.int32) for side in sides], at) > 0,
                pick([side.answers.astype(jnp.int32) for side in sides], at) > 0,
            )
        )
    return turned


def only_if(conditions, action):
    pl.when(functools.reduce(jnp.logical_and, conditions))(action)


def mixed(halved, rows):
    width = halved.shape[1] // 2
    return jnp.concatenate([halved[:, rows], halved[:, rows.start + width : rows.stop + width]], axis=1)


def kernel(
    sizes, cols_there, blocks,
    half, lhs, mix, far_edge, acc, sums, picks,
    cols, gates, own, far_diag, edge,
    cols_sem, load_sem, own_sem, sent, recv, ready,
):
    count = len(directions(sizes))
    kslots, block_size = own.shape[0], own.shape[1]
    size = block_size // 2
    top, bottom, whole = pl.ds(0, size), pl.ds(size, size), pl.ds(0, block_size)
    slots = pl.ds(1, kslots - 1)
    loads = [
        pltpu.make_async_copy(blocks.at[slots, rows], own.at[slots, rows], load_sem.at[k])
        for k, rows in enumerate((top, bottom))
    ]
    where_am_i = [lax.axis_index(name) for name in AXES]
    named_load = pltpu.make_async_copy(cols_there.at[where_am_i[0], where_am_i[1]], cols, cols_sem)
    loads[0].start()
    loads[1].start()
    strides = (sizes[1] * sizes[2], sizes[2], 1)
    low, high, pair, cross = sides_of(sizes, where_am_i)
    everyone = low + high + pair + cross
    swift = lax.rem(where_am_i[2], 2) == 0

    kinds = {id(side): k for k, sides in enumerate((low + high, pair, cross)) for side in sides}

    def kind(side):
        return kinds[id(side)] if id(side) in kinds else jnp.where(side.axis == 2, 2, 0)

    def copy(side, src, dst, at):
        return pltpu.make_async_remote_copy(
            src_ref=src,
            dst_ref=dst,
            send_sem=sent,
            recv_sem=recv.at[at],
            device_id=side.device,
            device_id_type=MESH,
        )

    def send_diag(side, src):
        return copy(side, src, far_diag.at[side.far_index], kind(side))

    def send_edge(side, rows):
        at = 3 + kind(side)
        if rows is bottom:
            at = jnp.where(kind(side) == 0, 6, at)
        return copy(side, edge.at[side.index, rows], far_edge.at[side.far_index, rows], at)

    def await_one(side, dst, at):
        only_if([side.there], lambda: copy(side, dst, dst, at).wait_recv())

    def number(sides):
        return sum((side.there.astype(jnp.int32) for side in sides), jnp.int32(0))

    def await_all(sides, dst, at):
        many = number(sides)
        for k in range(1, len(sides) + 1):
            part = dst(pl.ds(0, k))
            pl.when(many == k)(lambda part=part: copy(sides[0], part, part, at).wait_recv())

    def await_sent():
        many = number(everyone)
        for k in range(1, len(everyone) + 1):
            part = lhs.at[pl.ds(0, k)]
            pl.when(many == k)(lambda part=part: copy(everyone[0], part, part, 0).wait_send())

    def signal(side, semaphore):
        pl.semaphore_signal(semaphore, inc=1, device_id=side.device, device_id_type=MESH)

    barrier = pltpu.get_barrier_semaphore()
    for side in low + high + cross + pair:
        only_if(
            [side.there, jnp.logical_not(side.answers)], lambda side=side: signal(side, barrier)
        )
    peers = jnp.int32(0)
    for side in everyone:
        peers = peers + jnp.logical_and(side.there, side.answers).astype(jnp.int32)

    @pl.when(peers > 0)
    def _():
        pl.semaphore_wait(barrier, peers)

    for side in low + cross + pair:
        only_if([side.there, side.answers], lambda side=side: send_diag(side, blocks.at[0]).start())
    named_load.start()
    for side in low + cross + pair:
        only_if([side.there, side.answers], lambda side=side: signal(side, ready.at[kind(side)]))
    own_load = pltpu.make_async_copy(blocks.at[0], own.at[0], own_sem)
    own_load.start()
    for side in low + high + pair:

        @pl.when(jnp.logical_not(side.there))
        def _(side=side):
            far_diag[side.index] = jnp.zeros((block_size, block_size), jnp.float32)
            far_edge[side.index] = jnp.zeros((block_size, block_size), jnp.float32)

    def gather(side, found, rows):
        total = jnp.where(found[0], own[1, rows], 0.0)
        for s in range(2, kslots):
            total = total + jnp.where(found[s - 1], own[s, rows], 0.0)
        edge[side.index, rows] = total

    def name_of(side):
        return sum(place * stride for place, stride in zip(side.device, strides))

    turned = urgent_first(low + cross)
    urgent = turned[0]
    urgent_name = name_of(urgent)
    now = jnp.logical_and(urgent.there, urgent.answers)
    named_load.wait()
    named = [cols[where_am_i[2], s] for s in range(kslots)]
    found = [named[s] == urgent_name for s in range(1, kslots)]
    loads[0].wait()
    gather(urgent, found, top)
    only_if([now, jnp.logical_or(swift, urgent.axis == 2)], lambda: send_edge(urgent, top).start())
    loads[1].wait()
    gather(urgent, found, bottom)
    only_if(
        [now, jnp.logical_or(swift, urgent.axis == 2)], lambda: send_edge(urgent, bottom).start()
    )
    own_load.wait()
    named = [cols[where_am_i[2], s] for s in range(kslots)]
    for side in everyone:
        there = name_of(side)
        total = jnp.int32(0)
        for s in range(1, kslots):
            match = (named[s] == there).astype(jnp.int32)
            gates[side.index * kslots + s] = match
            total = total + match
        gates[side.index * kslots] = total

    def matches(side):
        return [gates[side.index * kslots + s] > 0 for s in range(1, kslots)]

    for side in turned[1:]:
        gather(side, matches(side), whole)
        now = jnp.logical_and(side.there, side.answers)
        only_if([now, jnp.logical_or(swift, side.axis == 2)], lambda side=side: send_edge(side, top).start())
        only_if(
            [now, jnp.logical_or(swift, side.axis == 2)], lambda side=side: send_edge(side, bottom).start()
        )
    for side in pair + high:
        gather(side, matches(side), whole)
        if side.axis == 2:
            only_if([side.there, side.answers], lambda side=side: send_edge(side, whole).start())
    def follow(side):
        send_diag(side, own.at[0]).start()
        if kind(side) == 1:
            send_edge(side, whole).start()
        else:
            send_edge(side, top).start()
            send_edge(side, bottom).start()

    greets = [jnp.logical_and(side.there, jnp.logical_not(side.answers)) for side in low + high]
    awaited = sum((greet.astype(jnp.int32) for greet in greets), jnp.int32(0))

    @pl.when(awaited > 0)
    def _():
        pl.semaphore_wait(ready.at[0], awaited)

    for side, greet in zip(low + high, greets):
        only_if([greet], lambda side=side: follow(side))
    for side in pair + cross:

        def answered(side=side):
            pl.semaphore_wait(ready.at[kind(side)], 1)
            follow(side)

        only_if([side.there, jnp.logical_not(side.answers)], answered)

    outer = functools.reduce(jnp.logical_or, [side.there for side in cross], jnp.bool_(False))

    def release(when):
        for side in low:

            def both_halves(side=side):
                send_edge(side, top).start()
                send_edge(side, bottom).start()

            only_if([side.there, side.answers, jnp.logical_not(swift), when], both_halves)

    half[...] = split(own[0])
    final = final_directions(sizes)
    for d in range(count):
        halved = split(edge[d])
        lhs[d, pl.ds(0, block_size)] = halved
        if d in final:
            mix[final.index(d), pl.ds(0, block_size), pl.ds(0, block_size)] = mixed(halved, slice(0, size))
            mix[final.index(d), pl.ds(0, block_size), pl.ds(block_size, block_size)] = mixed(
                halved, slice(size, block_size)
            )
    rights = [half[...]] + [lhs[d, pl.ds(0, block_size)] for d in range(count)]
    found = spread(half[...], rights)
    square = found[0]
    for d in range(count):
        acc[d] = found[1 + d]

    def diag_phase(group, then=lambda: None):
        if kind(group[0]) == 0:
            await_all(group, lambda part: far_diag.at[part], 0)
        else:
            await_one(group[0], far_diag.at[group[0].index], kind(group[0]))
        then()
        arrived = [twice(split(far_diag[side.index])) for side in group]
        near = [
            acc[side.index] + folded(dot(lhs[side.index, pl.ds(0, block_size)], right))
            for side, right in zip(group, arrived)
        ]
        for side, right, value in zip(group, arrived, near):
            repeats = gates[side.index * kslots].astype(jnp.float32)
            weighted = split(value * (-2.0 * repeats))
            if side.axis == 2:
                lhs[side.index, pl.ds(block_size, block_size)] = weighted
            else:
                at = final.index(side.index)
                mix[at, pl.ds(block_size, block_size), pl.ds(0, block_size)] = mixed(
                    weighted, slice(0, size)
                )
                mix[at, pl.ds(block_size, block_size), pl.ds(block_size, block_size)] = mixed(
                    weighted, slice(size, block_size)
                )
            acc[side.index] = 3.0 * value + folded(dot(weighted, right))

    lanes = lax.broadcasted_iota(jnp.int32, picks.shape, 0)
    picked = jnp.zeros(picks.shape, jnp.int32)
    for s in range(1, kslots):
        index = jnp.int32(1 + count)
        for side in everyone:
            index = jnp.where(matches(side)[s - 1], 1 + side.index, index)
        picked = jnp.where(lanes == s, index, picked)
    picks[...] = picked
    release(outer)
    diag_phase(pair, then=lambda: release(jnp.logical_not(outer)))
    sums[0] = square
    sums[1] = jnp.zeros((block_size, block_size), jnp.float32)

    def edge_phase(side):
        both = folded(dot(lhs[side.index], twice(split(far_edge[side.index]))))
        sums[0] += both[:block_size]
        sums[1] += both[block_size:]

    for side in pair:
        await_one(side, far_edge.at[side.index], 4)
        edge_phase(side)
    diag_phase(low + high)
    for side in cross:
        pl.when(side.there)(lambda side=side: diag_phase([side]))
    def first_halves(also):
        await_all(low + high, lambda part: far_edge.at[part, top], 3)
        for side in also:
            await_one(side, far_edge.at[side.index], 5)
        both = met(sizes, 0, mix, far_edge)
        for side in also:
            both += folded(dot(lhs[side.index], twice(split(far_edge[side.index]))))
        sums[0] += both[:block_size]
        sums[1] += both[block_size:]

    pl.when(outer)(lambda: first_halves(cross))
    pl.when(jnp.logical_not(outer))(lambda: first_halves([]))
    await_sent()
    await_all(low + high, lambda part: far_edge.at[part, bottom], 6)


def final_directions(sizes):
    return [d for d, (axis, _) in enumerate(directions(sizes)) if axis < 2]


def met(sizes, part, mix, far_edge):
    block_size = far_edge.shape[1]
    size = block_size // 2
    final = final_directions(sizes)
    left = [mix[k, :, pl.ds(part * block_size, block_size)] for k in range(len(final))]
    right = [twice(split(far_edge[d, pl.ds(part * size, size)])) for d in final]
    return folded(dot(jnp.concatenate(left, axis=1), jnp.concatenate(right, axis=0)))


def pairs_of(sizes):
    blocks = list(range(1 + len(directions(sizes))))
    return [blocks[at : at + 2] for at in range(0, len(blocks), 2)]


def finish(sizes, half, lhs, mix, far_edge, acc, sums, picks, out, res, sem):
    size = out.shape[1]
    held = 2 + (len(pairs_of(sizes)) + 1) // 2
    shapes = [(size // 2, 2 * size)] * 2 + [(size, 2 * size)] * (held - 2)
    pl.run_scoped(
        functools.partial(finish_on, sizes, half, lhs, mix, far_edge, acc, sums, picks, out, res, sem),
        *[pltpu.ACC(unit)(shape, jnp.float32) for unit in range(2) for shape in shapes],
    )


def finish_on(sizes, half, lhs, mix, far_edge, acc, sums, picks, out, res, sem, *held):
    count = len(directions(sizes))
    kslots, block_size = out.shape[0], out.shape[1]
    size = block_size // 2
    units = (held[: len(held) // 2], held[len(held) // 2 :])
    final = final_directions(sizes)
    lanes = pl.ds(block_size, block_size)

    def tiles(values, axis):
        blank = jnp.zeros_like(values[0])
        values = values + [blank] * (len(values) % 2)
        return [
            jnp.concatenate(values[at : at + 2], axis=axis) for at in range(0, len(values), 2)
        ]

    steps = tiles([twice(split(far_edge[d, pl.ds(size, size)])) for d in final], 0)
    rights = [half[...]] + [lhs[d, pl.ds(0, block_size)] for d in range(count)]
    pairs = pairs_of(sizes)
    work = ([], [])
    for p, pair in enumerate(pairs):
        for k, part in enumerate((slice(0, block_size), slice(block_size, 2 * block_size))):
            tile = twice(tiles([rights[b][:, part] for b in pair], 1)[0])
            unit = k if p == len(pairs) - 1 and len(pairs) % 2 else p % 2
            work[unit].append((p, tile))
    pushed = [0, 0]
    loaded = [0, 0]

    def push(unit, tile):
        pltpu.matmul_push_rhs(tile, staging_register=pushed[unit] % 2, mxu_index=unit)
        pushed[unit] += 1

    def multiply(unit, at, left, load):
        pltpu.matmul_acc_lhs(
            units[unit][at], left, load_staged_rhs=loaded[unit] % 2 if load else None
        )
        loaded[unit] += load

    queues = [steps + [tile for _, tile in work[unit]] for unit in range(2)]
    for unit in range(2):
        for tile in queues[unit][:2]:
            push(unit, tile)
    for k in range(len(steps)):
        for unit in range(2):
            for row in (0, block_size):
                left = tiles(
                    [mix[n, pl.ds(row + unit * size, size), lanes] for n in range(len(final))], 1
                )[k]
                multiply(unit, row // block_size, left, row == 0)
            if pushed[unit] < len(queues[unit]):
                push(unit, queues[unit][pushed[unit]])
    chosen = picks[...]
    index = [chosen[s, 0] for s in range(kslots)]
    near = [pltpu.matmul_pop(units[unit][0]) for unit in range(2)]
    square = sums[0] + folded(jnp.concatenate(near, axis=0))
    scaled = split(-2.0 * square)
    for unit in range(2):
        for p, _ in work[unit]:
            multiply(unit, 2 + p // 2, scaled, True)
            if pushed[unit] < len(queues[unit]):
                push(unit, queues[unit][pushed[unit]])
    far = [pltpu.matmul_pop(units[unit][1]) for unit in range(2)]
    cubed = sums[1] + folded(jnp.concatenate(far, axis=0))

    def write(s):
        pltpu.make_async_copy(res.at[index[s]], out.at[s], sem).start()

    res[1 + count] = jnp.zeros((block_size, block_size), jnp.float32)
    for s in range(1, kslots):
        pl.when(index[s] == 1 + count)(lambda s=s: write(s))
    for p, pair in enumerate(pairs):
        both = [
            pltpu.matmul_pop(units[unit][2 + p // 2])
            for unit in range(2)
            if any(p == other for other, _ in work[unit])
        ]
        value = both[0] if len(both) == 1 else both[0] + both[1]
        for k, b in enumerate(pair):
            base = 3.0 * square + cubed if b == 0 else acc[b - 1]
            res[b] = base + value[:, block_size * k : block_size * (k + 1)]
        if p == 0:
            pltpu.make_async_copy(res.at[0], out.at[0], sem).start()
        for s in range(1, kslots):
            mine = jnp.logical_and(index[s] >= max(pair[0], 1), index[s] <= pair[-1])
            pl.when(mine)(lambda s=s: write(s))
    pltpu.make_async_copy(out, out, sem).wait()


def on_device(sizes, blocks, columns):
    kslots, block_size = blocks.shape[3], blocks.shape[4]
    count = len(directions(sizes))
    block = (block_size, block_size)
    vmem, anywhere = pl.BlockSpec(memory_space=pltpu.VMEM), pl.BlockSpec(memory_space=pl.ANY)
    shared = pl.pallas_call(
        functools.partial(kernel, sizes),
        out_shape=[
            pltpu.VMEM((block_size, 2 * block_size), jnp.bfloat16),
            pltpu.VMEM((count, 2 * block_size, 2 * block_size), jnp.bfloat16),
            pltpu.VMEM((len(final_directions(sizes)), 2 * block_size, 2 * block_size), jnp.bfloat16),
            pltpu.VMEM((count,) + block, jnp.float32),
            pltpu.VMEM((count,) + block, jnp.float32),
            pltpu.VMEM((2,) + block, jnp.float32),
            pltpu.VMEM((kslots, 128), jnp.int32),
        ],
        in_specs=[anywhere, anywhere],
        out_specs=[vmem] * 7,
        scratch_shapes=[
            pltpu.SMEM(columns.shape[2:], jnp.int32),
            pltpu.SMEM((count * kslots,), jnp.int32),
            pltpu.VMEM((kslots,) + block, jnp.float32),
            pltpu.VMEM((count,) + block, jnp.float32),
            pltpu.VMEM((count,) + block, jnp.float32),
            pltpu.SemaphoreType.DMA,
            pltpu.SemaphoreType.DMA((2,)),
            pltpu.SemaphoreType.DMA,
            pltpu.SemaphoreType.DMA,
            pltpu.SemaphoreType.DMA((7,)),
            pltpu.SemaphoreType.REGULAR((3,)),
        ],
        compiler_params=pltpu.CompilerParams(collective_id=0, has_side_effects=True),
    )(columns, blocks.reshape((kslots,) + block))
    renewed = pl.pallas_call(
        functools.partial(finish, sizes),
        out_shape=jax.ShapeDtypeStruct((kslots,) + block, jnp.float32),
        in_specs=[vmem] * 7,
        out_specs=anywhere,
        scratch_shapes=[pltpu.VMEM((2 + count,) + block, jnp.float32), pltpu.SemaphoreType.DMA],
        compiler_params=pltpu.CompilerParams(),
    )(*[pltpu.with_memory_space_constraint(each, pltpu.VMEM) for each in shared])
    return renewed.reshape(blocks.shape)


def solution(mesh):
    sizes = tuple(mesh.shape[name] for name in AXES)
    return jax.shard_map(
        functools.partial(on_device, sizes),
        mesh=mesh,
        in_specs=(P("gx", "gy", "gz", None, None, None), P()),
        out_specs=P("gx", "gy", "gz", None, None, None),
        check_vma=False,
    )
```
